32 devices in a mesh: gx: 4 (over y, x), gy: 4 (over z), gz: 2 (over core).
Axes of the slice: x: 2, y: 2, z: 4, core: 2. Of those that a mesh axis runs over, the one named last changes fastest.
Arguments:
- node_positions: float32 [3, 32, 32, 512], P(None, 'gx', 'gy', 'gz'), may hold values from 0 to 4, as said below
- control_positions: float32 [3, 65536], P(None, ('gx', 'gy', 'gz')), may hold values from 0 to 4, as said below
- control_coefficient_values: float32 [3, 65536], P(None, ('gx', 'gy', 'gz')), may hold values from -2.4 to 2.4
- support_pairs: int32 [4096, 3], P(('gx', 'gy', 'gz')), may hold values from 0 to 31, as said below
- live_counts: int32 [32], P(('gx', 'gy', 'gz')), may hold values from 32 to 128
- sliver_flags: int32 [32, 32, 512], P('gx', 'gy', 'gz'), may hold values 0 or 1
Outputs:
- displacement: float32 [3, 32, 32, 512], P(None, 'gx', 'gy', 'gz')
The draws below stay inside these ranges and needn't reach their ends.
Inputs may be any that keep to these rules, and one draw needn't show every extreme that they name: `node_positions`: node coordinates lie within their node's cell of width 1 / 8, 1 / 8, 1 / 256 around the cell centre. `control_positions`: the control points of block o lie in the unit cube of that block. `support_pairs`: column 0 is a node tile below 32; column 1 is a block that differs from the row's own block by at most one along each of the three directions; column 2 is a slot below 4; slot p < 32 of every block names node tile p and the block itself.
All inputs are finite; a program needn't handle non-finite values. No bound on the sum of `sliver_flags` on one device may be relied on, other than what follows from the above.
Results may differ from the reference program's by a relative error of at most 0.0003.
Values sent between devices are 32-bit elements; how exact they have to be, the bound alone decides.
A program may use at most 64 MiB of HBM per device.

```python
import jax
import jax.numpy as jnp
from jax import lax

TILE = 512
CX = 8
CY = 8
CZ = 256
CT = 4
PAIRS = 128
SWEEPS = 2
NX = 32
NY = 32
NZ = 512
NTILES = 32
CTRL = 65536
N_GX = 4
N_GY = 4
N_GZ = 2
DEVICES = 32


def draw_node_positions(key, part):
    jitter = jax.random.uniform(key, (3, NX, NY, NZ), jnp.float32, -0.3, 0.3)
    index_x = jnp.arange(NX).astype(jnp.float32)[:, None, None]
    index_y = jnp.arange(NY).astype(jnp.float32)[None, :, None]
    index_z = jnp.arange(NZ).astype(jnp.float32)[None, None, :]
    coord_x = (index_x + 0.5 + jitter[0]) / CX
    coord_y = (index_y + 0.5 + jitter[1]) / CY
    coord_z = (index_z + 0.5 + jitter[2]) / CZ
    return jnp.stack([coord_x, coord_y, coord_z], 0).astype(jnp.float32)


def draw_control_positions(key, part):
    offsets = jax.random.uniform(key, (3, CTRL), jnp.float32, 0.0, 1.0)
    owner_ids = jnp.arange(CTRL) // (CT * TILE)
    block_x = (owner_ids // (N_GY * N_GZ)).astype(jnp.float32)
    block_y = (owner_ids // N_GZ % N_GY).astype(jnp.float32)
    block_z = (owner_ids % N_GZ).astype(jnp.float32)
    return jnp.stack([block_x + offsets[0], block_y + offsets[1], block_z + offsets[2]], 0).astype(jnp.float32)


def draw_support_pairs(key, part):
    key_tile = jax.random.fold_in(key, 11)
    key_step = jax.random.fold_in(key, 12)
    key_slot = jax.random.fold_in(key, 13)
    rows = DEVICES * PAIRS
    device_ids = jnp.arange(rows) // PAIRS
    slot_index = jnp.arange(rows) % PAIRS
    covering = slot_index < NTILES
    block_x = device_ids // (N_GY * N_GZ)
    block_y = device_ids // N_GZ % N_GY
    block_z = device_ids % N_GZ
    offsets = jax.random.randint(key_step, (rows, 3), -1, 2)
    offsets = jnp.where(covering[:, None], 0, offsets)
    owner_x = jnp.clip(block_x + offsets[:, 0], 0, N_GX - 1)
    owner_y = jnp.clip(block_y + offsets[:, 1], 0, N_GY - 1)
    owner_z = jnp.clip(block_z + offsets[:, 2], 0, N_GZ - 1)
    owner_ids = (owner_x * N_GY + owner_y) * N_GZ + owner_z
    tile_ids = jax.random.randint(key_tile, (rows,), 0, NTILES)
    tile_ids = jnp.where(covering, slot_index, tile_ids)
    slot_ids = jax.random.randint(key_slot, (rows,), 0, CT)
    return jnp.stack([tile_ids, owner_ids, slot_ids], 1).astype(jnp.int32)


def draw_live_counts(key, part):
    key_place = jax.random.fold_in(key, 21)
    key_load = jax.random.fold_in(key, 22)
    start_x = jax.random.randint(key_place, (), 0, N_GX - 1)
    device_ids = jnp.arange(DEVICES)
    block_x = device_ids // (N_GY * N_GZ)
    heavy = (block_x == start_x) | (block_x == start_x + 1)
    light_load = jax.random.randint(key_load, (DEVICES,), PAIRS // 4, PAIRS // 4 + PAIRS // 8 + 1)
    least_device = (start_x + 2) % N_GX * (N_GY * N_GZ)
    light_load = jnp.where(device_ids == least_device, PAIRS // 4, light_load)
    return jnp.where(heavy, PAIRS, light_load).astype(jnp.int32)


def plant(array, key, least, top_value):
    shape = array.shape
    spot = [jax.random.randint(jax.random.fold_in(key, axis), (), 0, shape[axis]) for axis in range(len(shape))]
    array = array.at[tuple(spot)].set(least)
    longest = shape.index(max(shape))
    spot[longest] = (spot[longest] + 1) % shape[longest]
    return array.at[tuple(spot)].set(top_value)


def steps_of(rng, dims, shards, low, top_value):
    loudness = 1.0
    for axis_at, parts in shards:
        steps = jax.random.uniform(jax.random.fold_in(jax.random.fold_in(rng, 6), axis_at), (parts,), jnp.float32, low / len(shards), top_value / len(shards))
        loudness = loudness * jnp.repeat(jnp.exp(steps), dims[axis_at] // parts).reshape((-1,) + (1,) * (len(dims) - 1 - axis_at))
    return loudness


def bell_draw(stream_key, extent, scale, bound, cuts=(), dtype=jnp.bfloat16):
    entries = scale * jax.random.normal(stream_key, extent, jnp.float32)
    if cuts:
        entries = entries * steps_of(stream_key, extent, cuts, -0.22, 0.18)
    return jnp.clip(entries, -bound, bound).astype(dtype)


def setup_inputs(seed: int = 0) -> dict:
    key_of = jax.random.split(jax.random.key(seed), 7)
    return {
        "node_positions": draw_node_positions(jax.random.fold_in(key_of[6], 71), 0),
        "control_positions": draw_control_positions(jax.random.fold_in(key_of[6], 71), 0),
        "control_coefficient_values": bell_draw(key_of[2], (3, CTRL), 0.3, 2.4, ((1, 32),), jnp.float32),
        "support_pairs": draw_support_pairs(jax.random.fold_in(key_of[6], 71), 0),
        "live_counts": draw_live_counts(jax.random.fold_in(key_of[6], 71), 0),
        "sliver_flags": plant((jax.random.randint(key_of[5], (NX, NY, NZ), 0, 4) < 1).astype(jnp.int32), jax.random.fold_in(key_of[5], 1), 0, 1),
    }


RADIUS = 1.5
OMEGA = 0.7

def kernel_sum(node_pos, source_node):
    dist_sq = jnp.zeros((node_pos.shape[1], node_pos.shape[2], source_node.shape[2]), jnp.float32)
    for axis_id in range(3):
        gap = node_pos[axis_id][:, :, None] - source_node[axis_id][:, None, :]
        dist_sq = dist_sq + gap * gap
    scaled = jnp.sqrt(dist_sq) / RADIUS
    falloff = jnp.maximum(1.0 - scaled, 0.0)
    kernel_weight = falloff * falloff * falloff * falloff * (4.0 * scaled + 1.0)
    return jnp.einsum('hpg,mhg->mhp', kernel_weight, source_node[3:], precision=lax.Precision.HIGHEST)

def relax_step(padded, flag_field):
    center = padded[:, 1:-1, 1:-1, 1:-1]
    neighbours = padded[:, 2:, 1:-1, 1:-1] + padded[:, :-2, 1:-1, 1:-1]
    neighbours = neighbours + padded[:, 1:-1, 2:, 1:-1] + padded[:, 1:-1, :-2, 1:-1]
    neighbours = neighbours + padded[:, 1:-1, 1:-1, 2:] + padded[:, 1:-1, 1:-1, :-2]
    return center + OMEGA * flag_field * (neighbours / 6.0 - center)

def reference(node_positions, control_positions, control_coefficient_values, support_pairs, live_counts, sliver_flags):
    devices = N_GX * N_GY * N_GZ
    node_grid = node_positions.reshape(3, N_GX, CX, N_GY, CY, N_GZ, CZ)
    node_grid = node_grid.transpose(1, 3, 5, 0, 2, 4, 6).reshape(devices, 3, NTILES, TILE)
    controls = jnp.concatenate([control_positions, control_coefficient_values], 0).reshape(6, devices * CT, TILE)
    pairing_table = support_pairs.reshape(devices, PAIRS, 3)

    def one_device(device_inputs):
        node_tiles, dev_pairs, live_count = device_inputs
        live_mask = (jnp.arange(PAIRS) < live_count).astype(jnp.float32)
        onehot = (dev_pairs[:, 0][:, None] == jnp.arange(NTILES)[None, :]).astype(jnp.float32) * live_mask[:, None]

        def one_pair(pair_row):
            node_pos = jnp.take(node_tiles, pair_row[0:1], axis=1)
            source_node = jnp.take(controls, (pair_row[1] * CT + pair_row[2]).reshape(1), axis=1)
            return kernel_sum(node_pos, source_node)[:, 0]
        contrib = lax.map(one_pair, dev_pairs)
        return jnp.einsum('pt,pcn->ctn', onehot, contrib, precision=lax.Precision.HIGHEST)
    displaced = lax.map(one_device, (node_grid, pairing_table, live_counts))
    displaced = displaced.reshape(N_GX, N_GY, N_GZ, 3, CX, CY, CZ).transpose(3, 0, 4, 1, 5, 2, 6).reshape(3, NX, NY, NZ)
    flag_field = sliver_flags.astype(jnp.float32)
    moved = displaced
    for sweep_counter_index in range(SWEEPS):
        padded = jnp.pad(moved, ((0, 0), (1, 1), (1, 1), (1, 1)))
        moved = relax_step(padded, flag_field)
    return moved
```

```python
import functools

import jax
import jax.numpy as jnp
from jax import lax
from jax.experimental import pallas as pl
from jax.experimental.pallas import tpu as pltpu
from jax.sharding import PartitionSpec as P

TILE = 512
CT = 4
PAIRS = 128
SWEEPS = 2
RADIUS = 1.5
OMEGA = 0.7
GROUP = 8
HALF = 256
FLOOR = 2.0**-21
bf16, f32 = jnp.bfloat16, jnp.float32


def split3(x):
    a = x.astype(bf16).astype(f32)
    r = x - a
    b = r.astype(bf16).astype(f32)
    return a, b, r - b


def row_ids():
    return lax.broadcasted_iota(jnp.int32, (8, TILE), 0)


def node_features(x_ref, t, origin):
    per = TILE // x_ref.shape[2]
    rows = row_ids()
    coords = []
    for c in range(3):
        row = jnp.concatenate(
            [x_ref[c, pl.ds(t * per + j, 1), :] for j in range(per)], axis=1
        )
        coords.append((row - origin[c]) * (1.0 / RADIUS))
    norm = coords[0] * coords[0] + coords[1] * coords[1] + coords[2] * coords[2]
    block = jnp.where(rows == 4, 1.0, 0.0)
    for i, row in enumerate(coords + [norm]):
        block = jnp.where(rows == i, jnp.broadcast_to(row, (8, TILE)), block)
    a, b, c = split3(block)
    return jnp.concatenate([a, a, b, b, a, c], 0).astype(bf16)


def control_features(raw, origin):
    rows = row_ids()
    shift = jnp.where(rows == 0, origin[0], jnp.where(rows == 1, origin[1], origin[2]))
    pos = jnp.where(rows < 3, (raw - shift) * (1.0 / RADIUS), 0.0)
    norm = jnp.sum(pos * pos, axis=0, keepdims=True) + FLOOR
    block = jnp.where(rows == 3, 1.0, -2.0 * pos)
    block = jnp.where(rows == 4, jnp.broadcast_to(norm, (8, TILE)), block)
    a, b, c = split3(block)
    return jnp.transpose(jnp.concatenate([a, b, a, b, c, a], 0)).astype(bf16)


def coef_parts(raw):
    high = raw.astype(bf16).astype(f32)
    return jnp.concatenate([high, raw - high], 0).astype(bf16)


def pair_sum(nodes, controls, coefs):
    coefs = jnp.concatenate([coefs, coefs], 1)
    sums = []
    for n in range(0, TILE, HALF):
        dist_sq = jnp.dot(controls, nodes[:, n : n + HALF], preferred_element_type=f32)
        scaled = dist_sq * lax.rsqrt(dist_sq)
        fall = jnp.maximum(1.0 - scaled, 0.0)
        fall2 = fall * fall
        weight = (fall2 * fall2) * (0.25 + scaled)
        top = weight.astype(bf16)
        rest = (weight - top.astype(f32)).astype(bf16)
        sums.append(
            jnp.dot(coefs, jnp.concatenate([top, rest], 0), preferred_element_type=f32)
        )
    return jnp.concatenate(sums, 1)


def peers(axis, shifts, wrap):
    count, me = lax.axis_size(axis), lax.axis_index(axis)
    for i, d in enumerate(shifts):
        if d == 0:
            continue
        step = d if wrap or d == 1 else d - count
        ahead = None if wrap else jnp.logical_and(me + step >= 0, me + step < count)
        behind = None if wrap else jnp.logical_and(me - step >= 0, me - step < count)
        yield i, (me + step + count) % count, (me - step + count) % count, ahead, behind


def when(cond, do):
    if cond is None:
        do()
    else:
        pl.when(cond)(do)


def gather_kernel(axes, half, slot_ref, live_ref, x_ref, pos_ref, coef_ref, pairs_ref, o_ref, table, x_both, mate_meta, own_ref, meta_ref, send, recv, extra, local, features, parts):
    origin = [lax.axis_index(axis).astype(f32) + 0.5 for axis, _, _ in axes]
    for s in range(CT):
        own_ref[s, 0:3] = pos_ref[:, s * TILE : (s + 1) * TILE]
        own_ref[s, 3:6] = coef_ref[:, s * TILE : (s + 1) * TILE]
        own_ref[s, 6:8] = jnp.zeros((2, TILE), f32)
    meta_ref[0:3] = pairs_ref[...]
    meta_ref[3:8] = jnp.full((5, meta_ref.shape[1]), live_ref[0], jnp.int32)
    barrier = pltpu.get_barrier_semaphore()
    expected = 0
    for axis, shifts, wrap in axes:
        for _, ahead, _, there, _ in peers(axis, shifts, wrap):
            when(there, lambda axis=axis, ahead=ahead: pl.semaphore_signal(
                barrier, inc=1, device_id={axis: ahead}, device_id_type=pl.DeviceIdType.MESH))
            expected = expected + (1 if there is None else there.astype(jnp.int32))
    pl.semaphore_wait(barrier, expected)

    def views(k, i):
        if k == 0:
            return own_ref, table.at[0, 0, i]
        if k == 1:
            return table.at[0, 0], table.at[0, i]
        return table.at[0], table.at[i]

    def copies(k):
        axis, shifts, wrap = axes[k]
        for i, ahead, behind, has_ahead, has_behind in peers(axis, shifts, wrap):
            src, dst = views(k, i)
            copy = pltpu.make_async_remote_copy(
                src_ref=src, dst_ref=dst, send_sem=send.at[k, i], recv_sem=recv.at[k, i],
                device_id={axis: behind}, device_id_type=pl.DeviceIdType.MESH)
            yield copy, has_behind, has_ahead

    def start(k):
        for copy, goes, _ in copies(k):
            when(goes, copy.start)

    def land(k):
        for copy, goes, comes in copies(k):
            when(comes, copy.wait_recv)
            when(goes, copy.wait_send)

    gx_name = axes[0][0]
    count = lax.axis_size(gx_name)
    mate = (lax.axis_index(gx_name) + half) % count
    keep = [
        pltpu.make_async_copy(own_ref, table.at[0, 0, 0], local.at[0]),
        pltpu.make_async_copy(x_ref, x_both.at[1], local.at[1]),
    ]
    for copy in keep:
        copy.start()
    start(0)
    swaps = [
        pltpu.make_async_remote_copy(
            src_ref=src, dst_ref=dst, send_sem=extra.at[0, n], recv_sem=extra.at[1, n],
            device_id={gx_name: mate}, device_id_type=pl.DeviceIdType.MESH)
        for n, (src, dst) in enumerate(((meta_ref, mate_meta), (x_ref, x_both.at[0])))
    ]
    swaps[0].start()

    groups = o_ref.shape[0] // GROUP

    for s in range(CT):
        features[s] = control_features(own_ref[s], origin)
        parts[s] = coef_parts(own_ref[s])

    cuts = [groups // 4, groups // 4 * 3, groups]

    @pl.loop(0, groups)
    def _(g):
        for j in range(GROUP):
            i = g * GROUP + j
            s = slot_ref[2, i]
            o_ref[i] = pair_sum(node_features(x_ref, i, origin), features[s], parts[s])
        for k in range(3):
            @pl.when(g == cuts[k] - 1)
            def _():
                if k == 0:
                    for copy in keep:
                        copy.wait()
                land(k)
                if k < 2:
                    start(k + 1)
                if k == 0:
                    swaps[1].start()

    for copy in swaps:
        copy.wait()


def finish(acc, at, o_ref):
    per = TILE // o_ref.shape[2]
    width = o_ref.shape[2]
    for t in range(o_ref.shape[1] // per):
        both = 4.0 * (acc[at + t, :8] + acc[at + t, 8:])
        for j in range(per):
            o_ref[:, t * per + j, :] = both[3:6, j * width : (j + 1) * width]


def rest_kernel(axes, half, meta, live, mate_meta, x_both, table, init, sent_ref, o_ref, acc):
    ntiles = init.shape[0]
    trash = 2 * ntiles
    acc[:ntiles] = jnp.zeros_like(init)
    acc[ntiles:trash] = init[...]
    here = [lax.axis_index(axis) for axis, _, _ in axes]
    counts = [lax.axis_size(axis) for axis, _, _ in axes]
    mate_at = lax.rem(here[0] + half, counts[0])
    mine, theirs = live[0], mate_meta[3, 0]
    goal = lax.div(mine + theirs + 1, 2)
    skip = jnp.minimum(goal, theirs)
    helped = theirs - skip
    total = helped + jnp.minimum(mine, goal) - ntiles

    def source(owner, slot):
        owners = (
            lax.div(owner, counts[1] * counts[2]),
            lax.rem(lax.div(owner, counts[2]), counts[1]),
            lax.rem(owner, counts[2]),
        )
        at = 0
        for k in (2, 1, 0):
            shifts = axes[k][1]
            rel = lax.rem(owners[k] - here[k] + counts[k], counts[k])
            at = at * len(shifts) + sum(jnp.where(rel == d, i, 0) for i, d in enumerate(shifts))
        return at * CT + slot

    @pl.loop(0, lax.div(total + GROUP - 1, GROUP))
    def _(g):
        for j in range(GROUP):
            p = g * GROUP + j
            for_mate = p < helped
            slot = jnp.minimum(jnp.where(for_mate, skip + p, ntiles + p - helped), PAIRS - 1)
            t, owner, tile = (
                jnp.where(for_mate, mate_meta[c, slot], meta[c, slot]) for c in range(3)
            )
            part = jnp.where(for_mate, 0, 1)
            origin = [
                jnp.where(for_mate, mate_at, here[0]).astype(f32) + 0.5,
                here[1].astype(f32) + 0.5,
                here[2].astype(f32) + 0.5,
            ]
            nodes = node_features(x_both.at[part], t, origin)
            into = jnp.where(p < total, part * ntiles + t, trash)
            raw = table[source(owner, tile)]
            acc[into] += pair_sum(nodes, control_features(raw, origin), coef_parts(raw))

    finish(acc, 0, sent_ref)
    finish(acc, ntiles, o_ref)


def smooth_kernel(half, sent_ref, mine_ref, flag_ref, o_ref, back, m, yface, xh, yh, zh, sems, zsend):
    names = ("gx", "gy", "gz")
    here = [lax.axis_index(a) for a in names]
    counts = [lax.axis_size(a) for a in names]
    mate = (here[0] + half) % counts[0]
    mesh_id = pl.DeviceIdType.MESH
    barrier = pltpu.get_barrier_semaphore()
    pl.semaphore_signal(barrier, inc=1, device_id={"gx": mate}, device_id_type=mesh_id)
    expected = 1
    faces = []
    for k, axis in enumerate(names):
        for side, step in enumerate((-1, 1)):
            at = here[k] + step
            there = jnp.logical_and(at >= 0, at < counts[k])
            at = jnp.clip(at, 0, counts[k] - 1)
            faces.append((k, side, axis, at, there))
            pl.when(there)(lambda axis=axis, at=at: pl.semaphore_signal(
                barrier, inc=1, device_id={axis: at}, device_id_type=mesh_id))
            expected = expected + there.astype(jnp.int32)
    pl.semaphore_wait(barrier, expected)
    swap = pltpu.make_async_remote_copy(
        src_ref=sent_ref, dst_ref=back, send_sem=sems.at[0, 2, 0, 0], recv_sem=sems.at[0, 2, 1, 0],
        device_id={"gx": mate}, device_id_type=mesh_id)
    swap.start()
    halos = (xh, yh, zh)
    for k, side, axis, at, there in faces:
        @pl.when(jnp.logical_not(there))
        def _():
            for r in range(SWEEPS):
                halos[k][r, side] = jnp.zeros(halos[k].shape[2:], f32)
    size_x, size_y, size_z = m.shape[2:]
    lanes = zh.shape[-1]
    weight = OMEGA * flag_ref[...].astype(f32)
    rows = lax.broadcasted_iota(jnp.int32, (size_x, size_y, size_z), 1)
    cols = lax.broadcasted_iota(jnp.int32, (size_x, size_y, size_z), 2)
    swap.wait()
    now = [mine_ref[c] + back[c] for c in range(3)]
    for r in range(SWEEPS):
        for c in range(3):
            m[r, c] = now[c]
            yface[r, 0, c] = now[c][:, 0, :]
            yface[r, 1, c] = now[c][:, size_y - 1, :]
        copies = []
        for k, side, axis, at, there in faces:
            if k == 0:
                src = m.at[r, :, (size_x - 1) * side]
            elif k == 1:
                src = yface.at[r, side]
            else:
                src = m.at[r, :, :, :, pl.ds((size_z - lanes) * side, lanes)]
            out = pltpu.make_async_remote_copy(
                src_ref=src, dst_ref=halos[k].at[r, 1 - side], send_sem=zsend.at[r, k, side],
                recv_sem=sems.at[r + 1, k, 1 - side, 0], device_id={axis: at}, device_id_type=mesh_id)
            back_in = pltpu.make_async_remote_copy(
                src_ref=src, dst_ref=halos[k].at[r, side], send_sem=zsend.at[r, k, side],
                recv_sem=sems.at[r + 1, k, side, 0], device_id={axis: at}, device_id_type=mesh_id)
            pl.when(there)(out.start)
            copies.append((out, back_in, there))
        for out, back_in, there in copies:
            pl.when(there)(back_in.wait_recv)
            pl.when(there)(out.wait_send)
        later = []
        for c in range(3):
            v = now[c]
            total = jnp.concatenate([xh[r, 0, c][None], v[:-1]], 0)
            total = total + jnp.concatenate([v[1:], xh[r, 1, c][None]], 0)
            low = jnp.broadcast_to(yh[r, 0, c][:, None, :], v.shape)
            high = jnp.broadcast_to(yh[r, 1, c][:, None, :], v.shape)
            total = total + jnp.where(rows == 0, low, pltpu.roll(v, 1, 1))
            total = total + jnp.where(rows == size_y - 1, high, pltpu.roll(v, size_y - 1, 1))
            low = pltpu.roll(zh[r, 0, c], 1, 2)
            high = pltpu.roll(zh[r, 1, c], lanes - 1, 2)
            low = jnp.concatenate([low] * (size_z // lanes), 2)
            high = jnp.concatenate([high] * (size_z // lanes), 2)
            total = total + jnp.where(cols == 0, low, pltpu.roll(v, 1, 2))
            total = total + jnp.where(cols == size_z - 1, high, pltpu.roll(v, size_z - 1, 2))
            later.append(v + weight * (total * (1.0 / 6.0) - v))
        now = later
    for c in range(3):
        o_ref[c] = now[c]


SM = pl.BlockSpec(memory_space=pltpu.SMEM)
VM = pl.BlockSpec(memory_space=pltpu.VMEM)


ANY = pl.BlockSpec(memory_space=pl.ANY)


def gather_call(axes, half, nodes, pos, coef, pairs, live):
    ntiles = nodes.shape[1] * nodes.shape[2] // TILE
    spans = [len(shifts) for _, shifts, _ in axes]
    widest = max(spans)
    return pl.pallas_call(
        functools.partial(gather_kernel, axes, half),
        out_shape=(
            jax.ShapeDtypeStruct((ntiles, 16, TILE), f32),
            jax.ShapeDtypeStruct((spans[2], spans[1], spans[0], CT, 8, TILE), f32),
            jax.ShapeDtypeStruct((2,) + nodes.shape, f32),
            jax.ShapeDtypeStruct((8, pairs.shape[1]), jnp.int32),
        ),
        in_specs=[SM, SM, VM, VM, VM, VM],
        out_specs=(VM, ANY, ANY, ANY),
        scratch_shapes=[
            pltpu.VMEM((CT, 8, TILE), f32),
            pltpu.VMEM((8, pairs.shape[1]), jnp.int32),
            pltpu.SemaphoreType.DMA((3, widest)),
            pltpu.SemaphoreType.DMA((3, widest)),
            pltpu.SemaphoreType.DMA((2, 2)),
            pltpu.SemaphoreType.DMA((2,)),
            pltpu.VMEM((CT, TILE, 48), bf16),
            pltpu.VMEM((CT, 16, TILE), bf16),
        ],
        compiler_params=pltpu.CompilerParams(collective_id=0, has_side_effects=True),
        name="gather",
    )(pairs, live, nodes, pos, coef, pairs)


def rest_call(axes, half, pairs, live, mate_meta, x_both, table, init):
    shape = jax.ShapeDtypeStruct(x_both.shape[1:], f32)
    return pl.pallas_call(
        functools.partial(rest_kernel, axes, half),
        out_shape=(shape, shape),
        in_specs=[SM, SM, SM, VM, VM, VM],
        out_specs=(VM, VM),
        scratch_shapes=[pltpu.VMEM((2 * init.shape[0] + 1, 16, TILE), f32)],
        name="rest",
    )(pairs, live, mate_meta, x_both, table, init)


def smooth_call(half, sent, mine, flags):
    shape = mine.shape
    _, size_x, size_y, size_z = shape
    lanes = min(128, size_z)
    return pl.pallas_call(
        functools.partial(smooth_kernel, half),
        out_shape=jax.ShapeDtypeStruct(shape, f32),
        in_specs=[VM, VM, VM],
        out_specs=VM,
        scratch_shapes=[
            pltpu.VMEM(shape, f32),
            pltpu.VMEM((SWEEPS,) + shape, f32),
            pltpu.VMEM((SWEEPS, 2, 3, size_x, size_z), f32),
            pltpu.VMEM((SWEEPS, 2, 3, size_y, size_z), f32),
            pltpu.VMEM((SWEEPS, 2, 3, size_x, size_z), f32),
            pltpu.VMEM((SWEEPS, 2, 3, size_x, size_y, lanes), f32),
            pltpu.SemaphoreType.DMA((SWEEPS + 1, 3, 2, 1)),
            pltpu.SemaphoreType.DMA((SWEEPS, 3, 2)),
        ],
        compiler_params=pltpu.CompilerParams(collective_id=1, has_side_effects=True),
        name="smooth",
    )(sent, mine, flags)


def offsets(count, wanted):
    seen = []
    for d in wanted:
        if d % count not in seen:
            seen.append(d % count)
    return seen


def on_device(
    node_positions,
    control_positions,
    control_coefficient_values,
    support_pairs,
    live_counts,
    sliver_flags,
):
    size_x, size_y, size_z = node_positions.shape[1:]
    nx, ny, nz = (lax.axis_size(a) for a in ("gx", "gy", "gz"))
    half = nx // 2
    nodes = node_positions.reshape(3, size_x * size_y, size_z)
    axes = (
        ("gx", offsets(nx, (0, 1, -1, half, half + 1, half - 1)), True),
        ("gy", offsets(ny, (0, 1, -1)), ny <= 2),
        ("gz", offsets(nz, (0, 1, -1)), nz <= 2),
    )
    pairs = support_pairs.T
    first, table, x_both, mate_meta = gather_call(
        axes, half, nodes, control_positions, control_coefficient_values, pairs, live_counts
    )
    table = table.reshape((-1,) + table.shape[4:])
    sent, mine = rest_call(axes, half, pairs, live_counts, mate_meta, x_both, table, first)
    shape = node_positions.shape
    return smooth_call(half, sent.reshape(shape), mine.reshape(shape), sliver_flags)


def solution(mesh):
    return jax.shard_map(
        on_device,
        mesh=mesh,
        in_specs=(
            P(None, "gx", "gy", "gz"),
            P(None, ("gx", "gy", "gz")),
            P(None, ("gx", "gy", "gz")),
            P(("gx", "gy", "gz"), None),
            P(("gx", "gy", "gz")),
            P("gx", "gy", "gz"),
        ),
        out_specs=P(None, "gx", "gy", "gz"),
        check_vma=False,
    )
```

```python
import functools

import jax
import jax.numpy as jnp
from jax import lax
from jax.experimental import pallas as pl
from jax.experimental.pallas import tpu as pltpu
from jax.sharding import PartitionSpec as P

TILE = 512
CT = 4
PAIRS = 128
SWEEPS = 2
RADIUS = 1.5
OMEGA = 0.7
GROUP = 8
STEP = 4
LATE = 8
HALF = 256
FLOOR = 2.0**-21
bf16, f32 = jnp.bfloat16, jnp.float32


def split3(x):
    a = x.astype(bf16).astype(f32)
    r = x - a
    b = r.astype(bf16).astype(f32)
    return a, b, r - b


def row_ids():
    return lax.broadcasted_iota(jnp.int32, (8, TILE), 0)


def node_features(x_ref, t, origin):
    per = TILE // x_ref.shape[2]
    rows = row_ids()
    coords = []
    for c in range(3):
        row = jnp.concatenate(
            [x_ref[c, pl.ds(t * per + j, 1), :] for j in range(per)], axis=1
        )
        coords.append((row - origin[c]) * (1.0 / RADIUS))
    norm = coords[0] * coords[0] + coords[1] * coords[1] + coords[2] * coords[2]
    block = jnp.where(rows == 4, 1.0, 0.0)
    for i, row in enumerate(coords + [norm]):
        block = jnp.where(rows == i, jnp.broadcast_to(row, (8, TILE)), block)
    a, b, c = split3(block)
    return jnp.concatenate([a, a, b, b, a, c], 0).astype(bf16)


def control_features(raw, origin):
    rows = row_ids()
    shift = jnp.where(rows == 0, origin[0], jnp.where(rows == 1, origin[1], origin[2]))
    pos = jnp.where(rows < 3, (raw - shift) * (1.0 / RADIUS), 0.0)
    norm = jnp.sum(pos * pos, axis=0, keepdims=True) + FLOOR
    block = jnp.where(rows == 3, 1.0, -2.0 * pos)
    block = jnp.where(rows == 4, jnp.broadcast_to(norm, (8, TILE)), block)
    a, b, c = split3(block)
    return jnp.transpose(jnp.concatenate([a, b, a, b, c, a], 0)).astype(bf16)


def coef_parts(raw):
    high = raw.astype(bf16).astype(f32)
    return jnp.concatenate([high, raw - high], 0).astype(bf16)


def pair_sum(nodes, controls, coefs):
    coefs = jnp.concatenate([coefs, coefs], 1)
    sums = []
    for n in range(0, TILE, HALF):
        dist_sq = jnp.dot(controls, nodes[:, n : n + HALF], preferred_element_type=f32)
        scaled = dist_sq * lax.rsqrt(dist_sq)
        fall = jnp.maximum(1.0 - scaled, 0.0)
        fall2 = fall * fall
        weight = (fall2 * fall2) * (0.25 + scaled)
        top = weight.astype(bf16)
        rest = (weight - top.astype(f32)).astype(bf16)
        sums.append(
            jnp.dot(coefs, jnp.concatenate([top, rest], 0), preferred_element_type=f32)
        )
    return jnp.concatenate(sums, 1)


def own_tiles(own_ref, pos_ref, coef_ref, features, parts, origin):
    for s in range(CT):
        own_ref[s, 0:3] = pos_ref[:, s * TILE : (s + 1) * TILE]
        own_ref[s, 3:6] = coef_ref[:, s * TILE : (s + 1) * TILE]
        own_ref[s, 6:8] = jnp.zeros((2, TILE), f32)
    for s in range(CT):
        features[s] = control_features(own_ref[s], origin)
        parts[s] = coef_parts(own_ref[s])


def merged(both):
    return 4.0 * (both[:8] + both[8:])


def peers(axis, shifts, wrap):
    count, me = lax.axis_size(axis), lax.axis_index(axis)
    for i, d in enumerate(shifts):
        if d == 0:
            continue
        step = d if wrap or d == 1 else d - count
        ahead = None if wrap else jnp.logical_and(me + step >= 0, me + step < count)
        behind = None if wrap else jnp.logical_and(me - step >= 0, me - step < count)
        yield i, (me + step + count) % count, (me - step + count) % count, ahead, behind


def both_of(a, b):
    if a is None or b is None:
        return b if a is None else a
    return jnp.logical_and(a, b)


def when(cond, do):
    if cond is None:
        do()
    else:
        pl.when(cond)(do)


def gather_kernel(axes, half, slot_ref, live_ref, x_ref, pos_ref, coef_ref, pairs_ref, o_ref, table, x_both, mate_meta, own_ref, meta_ref, send, recv, extra, local, features, parts):
    origin = [lax.axis_index(axis).astype(f32) + 0.5 for axis, _, _ in axes]
    own_tiles(own_ref, pos_ref, coef_ref, features, parts, origin)
    meta_ref[0:3] = pairs_ref[...]
    meta_ref[3:8] = jnp.full((5, meta_ref.shape[1]), live_ref[0], jnp.int32)
    barrier = pltpu.get_barrier_semaphore()
    expected = 0
    for axis, shifts, wrap in axes:
        for _, ahead, _, there, _ in peers(axis, shifts, wrap):
            when(there, lambda axis=axis, ahead=ahead: pl.semaphore_signal(
                barrier, inc=1, device_id={axis: ahead}, device_id_type=pl.DeviceIdType.MESH))
            expected = expected + (1 if there is None else there.astype(jnp.int32))
    pl.semaphore_wait(barrier, expected)

    wide = [len(shifts) for _, shifts, _ in axes]
    columns = [(i1, i0) for i1 in range(wide[1]) for i0 in range(wide[0])]
    came = {0: None}
    for i, _, _, has_ahead, _ in peers(*axes[1]):
        came[i] = has_ahead

    def copies(k, blocks):
        axis, shifts, wrap = axes[k]
        for i, ahead, behind, has_ahead, has_behind in peers(axis, shifts, wrap):
            for i1, i0 in blocks:
                src = table.at[0, i1, i0] if i1 or i0 else own_ref
                dst = table.at[(0, 0, i) if k == 0 else (0, i, i0) if k == 1 else (i, i1, i0)]
                n = i1 * wide[0] + i0
                copy = pltpu.make_async_remote_copy(
                    src_ref=src, dst_ref=dst, send_sem=send.at[k, i, n], recv_sem=recv.at[k, i, n],
                    device_id={axis: behind}, device_id_type=pl.DeviceIdType.MESH)
                yield copy, both_of(has_behind, came[i1]), both_of(has_ahead, came[i1])

    def start(k, blocks):
        for copy, goes, _ in copies(k, blocks):
            when(goes, copy.start)

    def land(k, blocks):
        for copy, goes, comes in copies(k, blocks):
            when(comes, copy.wait_recv)
            when(goes, copy.wait_send)

    near = [(0, 0)]
    row = [(0, i0) for i0 in range(1, wide[0])]
    side = [(i1, 0) for i1 in range(1, wide[1])]
    far = [(i1, i0) for i1, i0 in columns if i1 and i0]

    gx_name = axes[0][0]
    count = lax.axis_size(gx_name)
    mate = (lax.axis_index(gx_name) + half) % count
    keep = [
        pltpu.make_async_copy(own_ref, table.at[0, 0, 0], local.at[0]),
        pltpu.make_async_copy(x_ref, x_both.at[1], local.at[1]),
    ]
    for k in range(3):
        start(k, near)
    for copy in keep:
        copy.start()
    swaps = [
        pltpu.make_async_remote_copy(
            src_ref=src, dst_ref=dst, send_sem=extra.at[0, n], recv_sem=extra.at[1, n],
            device_id={gx_name: mate}, device_id_type=pl.DeviceIdType.MESH)
        for n, (src, dst) in enumerate(((meta_ref, mate_meta), (x_ref, x_both.at[0])))
    ]
    swaps[0].start()

    groups = o_ref.shape[0] // STEP

    @pl.loop(0, groups)
    def _(g):
        for j in range(STEP):
            i = g * STEP + j
            s = slot_ref[2, i]
            o_ref[i] = merged(pair_sum(node_features(x_ref, i, origin), features[s], parts[s]))

        @pl.when(g == groups // 3 - 1)
        def _():
            for copy in keep:
                copy.wait()
            land(0, near)
            start(1, row)
            land(1, near)
            start(2, row + side)
            swaps[1].start()

        @pl.when(g == groups - 2)
        def _():
            land(1, row)
            start(2, far)

    land(2, columns)
    for copy in swaps:
        copy.wait()


def finish(acc, at, o_ref):
    per = TILE // o_ref.shape[2]
    width = o_ref.shape[2]
    for t in range(o_ref.shape[1] // per):
        both = merged(acc[at + t])
        for j in range(per):
            o_ref[:, t * per + j, :] = both[3:6, j * width : (j + 1) * width]


def rest_kernel(axes, half, meta, live, mate_meta, x_both, table, sent_ref, o_ref, acc):
    trash = acc.shape[0] - 1
    ntiles = trash // 2
    acc[:trash] = jnp.zeros((trash,) + acc.shape[1:], f32)
    here = [lax.axis_index(axis) for axis, _, _ in axes]
    counts = [lax.axis_size(axis) for axis, _, _ in axes]
    mate_at = lax.rem(here[0] + half, counts[0])
    mine, theirs = live[0], mate_meta[3, 0]
    goal = lax.div(mine + theirs + 1, 2)
    skip = jnp.minimum(goal, theirs)
    helped = theirs - skip
    total = helped + jnp.minimum(mine, goal) - ntiles

    def source(owner, slot):
        owners = (
            lax.div(owner, counts[1] * counts[2]),
            lax.rem(lax.div(owner, counts[2]), counts[1]),
            lax.rem(owner, counts[2]),
        )
        at = 0
        for k in (2, 1, 0):
            shifts = axes[k][1]
            rel = lax.rem(owners[k] - here[k] + counts[k], counts[k])
            at = at * len(shifts) + sum(jnp.where(rel == d, i, 0) for i, d in enumerate(shifts))
        return at * CT + slot

    @pl.loop(0, lax.div(total + GROUP - 1, GROUP))
    def _(g):
        for j in range(GROUP):
            p = g * GROUP + j
            for_mate = p < helped
            slot = jnp.minimum(jnp.where(for_mate, skip + p, ntiles + p - helped), PAIRS - 1)
            t, owner, tile = (
                jnp.where(for_mate, mate_meta[c, slot], meta[c, slot]) for c in range(3)
            )
            part = jnp.where(for_mate, 0, 1)
            origin = [
                jnp.where(for_mate, mate_at, here[0]).astype(f32) + 0.5,
                here[1].astype(f32) + 0.5,
                here[2].astype(f32) + 0.5,
            ]
            nodes = node_features(x_both.at[part], t, origin)
            into = jnp.where(p < total, part * ntiles + t, trash)
            raw = table[source(owner, tile)]
            acc[into] += pair_sum(nodes, control_features(raw, origin), coef_parts(raw))

    finish(acc, 0, sent_ref)
    finish(acc, ntiles, o_ref)


def smooth_kernel(half, slot_ref, x_ref, pos_ref, coef_ref, first_ref, sent_ref, mine_ref, flag_ref, o_ref, back, m, yface, xh, yh, zh, sems, zsend, own_ref, features, parts, rbf):
    names = ("gx", "gy", "gz")
    here = [lax.axis_index(a) for a in names]
    counts = [lax.axis_size(a) for a in names]
    mate = (here[0] + half) % counts[0]
    mesh_id = pl.DeviceIdType.MESH
    barrier = pltpu.get_barrier_semaphore()
    pl.semaphore_signal(barrier, inc=1, device_id={"gx": mate}, device_id_type=mesh_id)
    expected = 1
    faces = []
    for k, axis in enumerate(names):
        for side, step in enumerate((-1, 1)):
            at = here[k] + step
            there = jnp.logical_and(at >= 0, at < counts[k])
            at = jnp.clip(at, 0, counts[k] - 1)
            faces.append((k, side, axis, at, there))
            pl.when(there)(lambda axis=axis, at=at: pl.semaphore_signal(
                barrier, inc=1, device_id={axis: at}, device_id_type=mesh_id))
            expected = expected + there.astype(jnp.int32)
    pl.semaphore_wait(barrier, expected)
    swap = pltpu.make_async_remote_copy(
        src_ref=sent_ref, dst_ref=back, send_sem=sems.at[0, 2, 0, 0], recv_sem=sems.at[0, 2, 1, 0],
        device_id={"gx": mate}, device_id_type=mesh_id)
    swap.start()
    halos = (xh, yh, zh)
    for k, side, axis, at, there in faces:
        @pl.when(jnp.logical_not(there))
        def _():
            for r in range(SWEEPS):
                halos[k][r, side] = jnp.zeros(halos[k].shape[2:], f32)
    size_x, size_y, size_z = m.shape[2:]
    lanes = zh.shape[-1]
    weight = OMEGA * flag_ref[...].astype(f32)
    origin = [at.astype(f32) + 0.5 for at in here]
    own_tiles(own_ref, pos_ref, coef_ref, features, parts, origin)
    per = TILE // size_z
    early = first_ref.shape[0]
    for t in range(early + LATE):
        if t < early:
            both = first_ref[t]
        else:
            s = slot_ref[2, t]
            both = merged(pair_sum(node_features(x_ref, t, origin), features[s], parts[s]))
        for j in range(per):
            at = t * per + j
            rbf[:, at // size_y, at % size_y, :] = both[3:6, j * size_z : (j + 1) * size_z]
    rows = lax.broadcasted_iota(jnp.int32, (size_x, size_y, size_z), 1)
    cols = lax.broadcasted_iota(jnp.int32, (size_x, size_y, size_z), 2)
    swap.wait()
    now = [rbf[c] + (mine_ref[c] + back[c]) for c in range(3)]
    for r in range(SWEEPS):
        for c in range(3):
            m[r, c] = now[c]
            yface[r, 0, c] = now[c][:, 0, :]
            yface[r, 1, c] = now[c][:, size_y - 1, :]
        copies = []
        for k, side, axis, at, there in faces:
            if k == 0:
                src = m.at[r, :, (size_x - 1) * side]
            elif k == 1:
                src = yface.at[r, side]
            else:
                src = m.at[r, :, :, :, pl.ds((size_z - lanes) * side, lanes)]
            out = pltpu.make_async_remote_copy(
                src_ref=src, dst_ref=halos[k].at[r, 1 - side], send_sem=zsend.at[r, k, side],
                recv_sem=sems.at[r + 1, k, 1 - side, 0], device_id={axis: at}, device_id_type=mesh_id)
            back_in = pltpu.make_async_remote_copy(
                src_ref=src, dst_ref=halos[k].at[r, side], send_sem=zsend.at[r, k, side],
                recv_sem=sems.at[r + 1, k, side, 0], device_id={axis: at}, device_id_type=mesh_id)
            pl.when(there)(out.start)
            copies.append((out, back_in, there))
        for out, back_in, there in copies:
            pl.when(there)(back_in.wait_recv)
            pl.when(there)(out.wait_send)
        later = []
        for c in range(3):
            v = now[c]
            total = jnp.concatenate([xh[r, 0, c][None], v[:-1]], 0)
            total = total + jnp.concatenate([v[1:], xh[r, 1, c][None]], 0)
            low = jnp.broadcast_to(yh[r, 0, c][:, None, :], v.shape)
            high = jnp.broadcast_to(yh[r, 1, c][:, None, :], v.shape)
            total = total + jnp.where(rows == 0, low, pltpu.roll(v, 1, 1))
            total = total + jnp.where(rows == size_y - 1, high, pltpu.roll(v, size_y - 1, 1))
            low = pltpu.roll(zh[r, 0, c], 1, 2)
            high = pltpu.roll(zh[r, 1, c], lanes - 1, 2)
            low = jnp.concatenate([low] * (size_z // lanes), 2)
            high = jnp.concatenate([high] * (size_z // lanes), 2)
            total = total + jnp.where(cols == 0, low, pltpu.roll(v, 1, 2))
            total = total + jnp.where(cols == size_z - 1, high, pltpu.roll(v, size_z - 1, 2))
            later.append(v + weight * (total * (1.0 / 6.0) - v))
        now = later
    for c in range(3):
        o_ref[c] = now[c]


SM = pl.BlockSpec(memory_space=pltpu.SMEM)
VM = pl.BlockSpec(memory_space=pltpu.VMEM)


ANY = pl.BlockSpec(memory_space=pl.ANY)


def gather_call(axes, half, nodes, pos, coef, pairs, live):
    ntiles = nodes.shape[1] * nodes.shape[2] // TILE
    spans = [len(shifts) for _, shifts, _ in axes]
    widest = max(spans)
    return pl.pallas_call(
        functools.partial(gather_kernel, axes, half),
        out_shape=(
            jax.ShapeDtypeStruct((ntiles - LATE, 8, TILE), f32),
            jax.ShapeDtypeStruct((spans[2], spans[1], spans[0], CT, 8, TILE), f32),
            jax.ShapeDtypeStruct((2,) + nodes.shape, f32),
            jax.ShapeDtypeStruct((8, pairs.shape[1]), jnp.int32),
        ),
        in_specs=[SM, SM, VM, VM, VM, VM],
        out_specs=(VM, ANY, ANY, ANY),
        scratch_shapes=[
            pltpu.VMEM((CT, 8, TILE), f32),
            pltpu.VMEM((8, pairs.shape[1]), jnp.int32),
            pltpu.SemaphoreType.DMA((3, widest, spans[0] * spans[1])),
            pltpu.SemaphoreType.DMA((3, widest, spans[0] * spans[1])),
            pltpu.SemaphoreType.DMA((2, 2)),
            pltpu.SemaphoreType.DMA((2,)),
            pltpu.VMEM((CT, TILE, 48), bf16),
            pltpu.VMEM((CT, 16, TILE), bf16),
        ],
        compiler_params=pltpu.CompilerParams(collective_id=0, has_side_effects=True),
        name="gather",
    )(pairs, live, nodes, pos, coef, pairs)


def rest_call(axes, half, pairs, live, mate_meta, x_both, table):
    ntiles = x_both.shape[2] * x_both.shape[3] // TILE
    shape = jax.ShapeDtypeStruct(x_both.shape[1:], f32)
    return pl.pallas_call(
        functools.partial(rest_kernel, axes, half),
        out_shape=(shape, shape),
        in_specs=[SM, SM, SM, VM, VM],
        out_specs=(VM, VM),
        scratch_shapes=[pltpu.VMEM((2 * ntiles + 1, 16, TILE), f32)],
        name="rest",
    )(pairs, live, mate_meta, x_both, table)


def smooth_call(half, pairs, nodes, pos, coef, first, sent, mine, flags):
    shape = mine.shape
    _, size_x, size_y, size_z = shape
    lanes = min(128, size_z)
    return pl.pallas_call(
        functools.partial(smooth_kernel, half),
        out_shape=jax.ShapeDtypeStruct(shape, f32),
        in_specs=[SM] + [VM] * 7,
        out_specs=VM,
        scratch_shapes=[
            pltpu.VMEM(shape, f32),
            pltpu.VMEM((SWEEPS,) + shape, f32),
            pltpu.VMEM((SWEEPS, 2, 3, size_x, size_z), f32),
            pltpu.VMEM((SWEEPS, 2, 3, size_y, size_z), f32),
            pltpu.VMEM((SWEEPS, 2, 3, size_x, size_z), f32),
            pltpu.VMEM((SWEEPS, 2, 3, size_x, size_y, lanes), f32),
            pltpu.SemaphoreType.DMA((SWEEPS + 1, 3, 2, 1)),
            pltpu.SemaphoreType.DMA((SWEEPS, 3, 2)),
            pltpu.VMEM((CT, 8, TILE), f32),
            pltpu.VMEM((CT, TILE, 48), bf16),
            pltpu.VMEM((CT, 16, TILE), bf16),
            pltpu.VMEM(shape, f32),
        ],
        compiler_params=pltpu.CompilerParams(collective_id=1, has_side_effects=True),
        name="smooth",
    )(pairs, nodes, pos, coef, first, sent, mine, flags)


def offsets(count, wanted):
    seen = []
    for d in wanted:
        if d % count not in seen:
            seen.append(d % count)
    return seen


def on_device(
    node_positions,
    control_positions,
    control_coefficient_values,
    support_pairs,
    live_counts,
    sliver_flags,
):
    size_x, size_y, size_z = node_positions.shape[1:]
    nx, ny, nz = (lax.axis_size(a) for a in ("gx", "gy", "gz"))
    half = nx // 2
    nodes = node_positions.reshape(3, size_x * size_y, size_z)
    axes = (
        ("gx", offsets(nx, (0, 1, -1, half, half + 1, half - 1)), True),
        ("gy", offsets(ny, (0, 1, -1)), ny <= 2),
        ("gz", offsets(nz, (0, 1, -1)), nz <= 2),
    )
    pairs = support_pairs.T
    first, table, x_both, mate_meta = gather_call(
        axes, half, nodes, control_positions, control_coefficient_values, pairs, live_counts
    )
    table = table.reshape((-1,) + table.shape[4:])
    sent, mine = rest_call(axes, half, pairs, live_counts, mate_meta, x_both, table)
    shape = node_positions.shape
    return smooth_call(
        half, pairs, nodes, control_positions, control_coefficient_values, first,
        sent.reshape(shape), mine.reshape(shape), sliver_flags,
    )


def solution(mesh):
    return jax.shard_map(
        on_device,
        mesh=mesh,
        in_specs=(
            P(None, "gx", "gy", "gz"),
            P(None, ("gx", "gy", "gz")),
            P(None, ("gx", "gy", "gz")),
            P(("gx", "gy", "gz"), None),
            P(("gx", "gy", "gz")),
            P("gx", "gy", "gz"),
        ),
        out_specs=P(None, "gx", "gy", "gz"),
        check_vma=False,
    )
```

```python
import functools

import jax
import jax.numpy as jnp
from jax import lax
from jax.experimental import pallas as pl
from jax.experimental.pallas import tpu as pltpu
from jax.sharding import PartitionSpec as P

TILE = 512
CT = 4
PAIRS = 128
SWEEPS = 2
RADIUS = 1.5
OMEGA = 0.7
GROUP = 8
STEP = 4
LATE = 12
HALF = 256
FLOOR = 2.0**-21
bf16, f32 = jnp.bfloat16, jnp.float32


def split3(x):
    a = x.astype(bf16).astype(f32)
    r = x - a
    b = r.astype(bf16).astype(f32)
    return a, b, r - b


def row_ids():
    return lax.broadcasted_iota(jnp.int32, (8, TILE), 0)


def node_features(x_ref, t, origin):
    per = TILE // x_ref.shape[2]
    rows = row_ids()
    coords = []
    for c in range(3):
        row = jnp.concatenate(
            [x_ref[c, pl.ds(t * per + j, 1), :] for j in range(per)], axis=1
        )
        coords.append((row - origin[c]) * (1.0 / RADIUS))
    norm = coords[0] * coords[0] + coords[1] * coords[1] + coords[2] * coords[2]
    block = jnp.where(rows == 4, 1.0, 0.0)
    for i, row in enumerate(coords + [norm]):
        block = jnp.where(rows == i, jnp.broadcast_to(row, (8, TILE)), block)
    a, b, c = split3(block)
    return jnp.concatenate([a, a, b, b, a, c], 0).astype(bf16)


def control_features(raw, origin):
    rows = row_ids()
    shift = jnp.where(rows == 0, origin[0], jnp.where(rows == 1, origin[1], origin[2]))
    pos = jnp.where(rows < 3, (raw - shift) * (1.0 / RADIUS), 0.0)
    norm = jnp.sum(pos * pos, axis=0, keepdims=True) + FLOOR
    block = jnp.where(rows == 3, 1.0, -2.0 * pos)
    block = jnp.where(rows == 4, jnp.broadcast_to(norm, (8, TILE)), block)
    a, b, c = split3(block)
    return jnp.transpose(jnp.concatenate([a, b, a, b, c, a], 0)).astype(bf16)


def coef_parts(raw):
    high = raw.astype(bf16).astype(f32)
    return jnp.concatenate([high, raw - high], 0).astype(bf16)


def pair_sum(nodes, controls, coefs):
    coefs = jnp.concatenate([coefs, coefs], 1)
    sums = []
    for n in range(0, TILE, HALF):
        dist_sq = jnp.dot(controls, nodes[:, n : n + HALF], preferred_element_type=f32)
        scaled = dist_sq * lax.rsqrt(dist_sq)
        fall = jnp.maximum(1.0 - scaled, 0.0)
        fall2 = fall * fall
        weight = (fall2 * fall2) * (0.25 + scaled)
        top = weight.astype(bf16)
        rest = (weight - top.astype(f32)).astype(bf16)
        sums.append(
            jnp.dot(coefs, jnp.concatenate([top, rest], 0), preferred_element_type=f32)
        )
    return jnp.concatenate(sums, 1)


def own_tiles(pos_ref, coef_ref, features, parts, origin):
    for s in range(CT):
        at = slice(s * TILE, (s + 1) * TILE)
        raw = jnp.concatenate([pos_ref[:, at], coef_ref[:, at], jnp.zeros((2, TILE), f32)], 0)
        features[s] = control_features(raw, origin)
        parts[s] = coef_parts(raw)


def pack_tiles(pos_ref, coef_ref, own_ref):
    last = slice((CT - 1) * TILE, CT * TILE)
    for s in range(CT - 1):
        at = slice(s * TILE, (s + 1) * TILE)
        own_ref[s, 0:3] = pos_ref[:, at]
        own_ref[s, 3:6] = coef_ref[:, at]
        for j in range(2):
            c = 2 * s + j
            own_ref[s, 6 + j : 7 + j] = pos_ref[c : c + 1, last] if c < 3 else coef_ref[c - 3 : c - 2, last]


def tile_rows(table, block, slot):
    first = block * (CT - 1)
    whole = table[first + jnp.minimum(slot, CT - 2)]
    last = jnp.concatenate([table[first + s, 6:8] for s in range(CT - 1)] + [jnp.zeros((2, TILE), f32)], 0)
    return jnp.where(slot == CT - 1, last, whole)


def merged(both):
    return 4.0 * (both[:8] + both[8:])


def peers(axis, shifts, wrap):
    count, me = lax.axis_size(axis), lax.axis_index(axis)
    for i, d in enumerate(shifts):
        if d == 0:
            continue
        step = d if wrap or d == 1 else d - count
        ahead = None if wrap else jnp.logical_and(me + step >= 0, me + step < count)
        behind = None if wrap else jnp.logical_and(me - step >= 0, me - step < count)
        yield i, (me + step + count) % count, (me - step + count) % count, ahead, behind


def both_of(a, b):
    if a is None or b is None:
        return b if a is None else a
    return jnp.logical_and(a, b)


def when(cond, do):
    if cond is None:
        do()
    else:
        pl.when(cond)(do)


def gather_kernel(axes, half, slot_ref, live_ref, x_ref, pos_ref, coef_ref, pairs_ref, o_ref, table, x_both, mate_meta, own_ref, meta_ref, send, recv, extra, local, features, parts):
    origin = [lax.axis_index(axis).astype(f32) + 0.5 for axis, _, _ in axes]
    barrier = pltpu.get_barrier_semaphore()
    expected = 0
    for axis, shifts, wrap in axes:
        for _, ahead, _, there, _ in peers(axis, shifts, wrap):
            when(there, lambda axis=axis, ahead=ahead: pl.semaphore_signal(
                barrier, inc=1, device_id={axis: ahead}, device_id_type=pl.DeviceIdType.MESH))
            expected = expected + (1 if there is None else there.astype(jnp.int32))
    meta_ref[0:3] = pairs_ref[...]
    meta_ref[3:8] = jnp.full((5, meta_ref.shape[1]), live_ref[0], jnp.int32)
    pack_tiles(pos_ref, coef_ref, own_ref)
    pl.semaphore_wait(barrier, expected)

    wide = [len(shifts) for _, shifts, _ in axes]
    columns = [(i1, i0) for i1 in range(wide[1]) for i0 in range(wide[0])]
    came = {0: None}
    for i, _, _, has_ahead, _ in peers(*axes[1]):
        came[i] = has_ahead

    def copies(k, blocks, only=None):
        axis, shifts, wrap = axes[k]
        for i, ahead, behind, has_ahead, has_behind in peers(axis, shifts, wrap):
            for i1, i0 in blocks if only is None or i in only else ():
                src = table.at[0, i1, i0] if i1 or i0 else own_ref
                dst = table.at[(0, 0, i) if k == 0 else (0, i, i0) if k == 1 else (i, i1, i0)]
                n = i1 * wide[0] + i0
                copy = pltpu.make_async_remote_copy(
                    src_ref=src, dst_ref=dst, send_sem=send.at[k, i, n], recv_sem=recv.at[k, i, n],
                    device_id={axis: behind}, device_id_type=pl.DeviceIdType.MESH)
                yield copy, both_of(has_behind, came[i1]), both_of(has_ahead, came[i1])

    def start(k, blocks):
        for copy, goes, _ in copies(k, blocks):
            when(goes, copy.start)

    def land(k, blocks, only=None):
        for copy, _, comes in copies(k, blocks, only):
            when(comes, copy.wait_recv)

    def drain(k, blocks):
        for copy, goes, _ in copies(k, blocks):
            when(goes, copy.wait_send)

    def relay(i0):
        land(0, near, (i0,))
        start(1, [(0, i0)])
        start(2, [(0, i0)])

    near = [(0, 0)]
    row = [(0, i0) for i0 in range(1, wide[0])]
    side = [(i1, 0) for i1 in range(1, wide[1])]

    gx_name = axes[0][0]
    count = lax.axis_size(gx_name)
    mate = (lax.axis_index(gx_name) + half) % count
    keep = [
        pltpu.make_async_copy(own_ref, table.at[0, 0, 0], local.at[0]),
        pltpu.make_async_copy(x_ref, x_both.at[1], local.at[1]),
    ]
    for k in range(3):
        start(k, near)
    for copy in keep:
        copy.start()
    swaps = [
        pltpu.make_async_remote_copy(
            src_ref=src, dst_ref=dst, send_sem=extra.at[0, n], recv_sem=extra.at[1, n],
            device_id={gx_name: mate}, device_id_type=pl.DeviceIdType.MESH)
        for n, (src, dst) in enumerate(((meta_ref, mate_meta), (x_ref, x_both.at[0])))
    ]
    swaps[0].start()

    own_tiles(pos_ref, coef_ref, features, parts, origin)
    groups = o_ref.shape[0] // STEP
    direct = [i for i, d in enumerate(axes[0][1]) if d == half]
    others = [i for i in range(1, wide[0]) if i not in direct]

    @pl.loop(0, groups)
    def _(g):
        for j in range(STEP):
            i = g * STEP + j
            s = slot_ref[2, i]
            o_ref[i] = merged(pair_sum(node_features(x_ref, i, origin), features[s], parts[s]))

        @pl.when(g == 1)
        def _():
            for i0 in direct + others:
                relay(i0)
            swaps[1].start()
            for copy in keep:
                copy.wait()
            land(1, near)
            start(2, side)

        @pl.when(g == 3)
        def _():
            for i0 in direct + others:
                land(1, [(0, i0)])
                start(2, [(i1, i0) for i1 in range(1, wide[1])])

    land(2, columns)
    drain(0, near)
    drain(1, near + row)
    drain(2, columns)
    for copy in swaps:
        copy.wait()


def finish(acc, at, o_ref):
    per = TILE // o_ref.shape[2]
    width = o_ref.shape[2]
    for t in range(o_ref.shape[1] // per):
        both = merged(acc[at + t])
        for j in range(per):
            o_ref[:, t * per + j, :] = both[3:6, j * width : (j + 1) * width]


def rest_kernel(axes, half, meta, live, mate_meta, x_both, table, sent_ref, o_ref, acc):
    trash = acc.shape[0] - 1
    ntiles = trash // 2
    acc[:trash] = jnp.zeros((trash,) + acc.shape[1:], f32)
    here = [lax.axis_index(axis) for axis, _, _ in axes]
    counts = [lax.axis_size(axis) for axis, _, _ in axes]
    mate_at = lax.rem(here[0] + half, counts[0])
    mine, theirs = live[0], mate_meta[3, 0]
    goal = lax.div(mine + theirs + 1, 2)
    skip = jnp.minimum(goal, theirs)
    helped = theirs - skip
    total = helped + jnp.minimum(mine, goal) - ntiles

    def source(owner):
        owners = (
            lax.div(owner, counts[1] * counts[2]),
            lax.rem(lax.div(owner, counts[2]), counts[1]),
            lax.rem(owner, counts[2]),
        )
        at = 0
        for k in (2, 1, 0):
            shifts = axes[k][1]
            rel = lax.rem(owners[k] - here[k] + counts[k], counts[k])
            at = at * len(shifts) + sum(jnp.where(rel == d, i, 0) for i, d in enumerate(shifts))
        return at

    @pl.loop(0, lax.div(total + GROUP - 1, GROUP))
    def _(g):
        for j in range(GROUP):
            p = g * GROUP + j
            for_mate = p < helped
            slot = jnp.minimum(jnp.where(for_mate, skip + p, ntiles + p - helped), PAIRS - 1)
            t, owner, tile = (
                jnp.where(for_mate, mate_meta[c, slot], meta[c, slot]) for c in range(3)
            )
            part = jnp.where(for_mate, 0, 1)
            origin = [
                jnp.where(for_mate, mate_at, here[0]).astype(f32) + 0.5,
                here[1].astype(f32) + 0.5,
                here[2].astype(f32) + 0.5,
            ]
            nodes = node_features(x_both.at[part], t, origin)
            into = jnp.where(p < total, part * ntiles + t, trash)
            raw = tile_rows(table, source(owner), tile)
            acc[into] += pair_sum(nodes, control_features(raw, origin), coef_parts(raw))

    finish(acc, 0, sent_ref)
    finish(acc, ntiles, o_ref)


def smooth_kernel(half, slot_ref, x_ref, pos_ref, coef_ref, first_ref, sent_ref, mine_ref, flag_ref, o_ref, back, m, yface, xh, yh, zh, sems, zsend, features, parts, rbf):
    names = ("gx", "gy", "gz")
    here = [lax.axis_index(a) for a in names]
    counts = [lax.axis_size(a) for a in names]
    mate = (here[0] + half) % counts[0]
    mesh_id = pl.DeviceIdType.MESH
    barrier = pltpu.get_barrier_semaphore()
    pl.semaphore_signal(barrier, inc=1, device_id={"gx": mate}, device_id_type=mesh_id)
    expected = 1
    faces = []
    for k, axis in enumerate(names):
        for side, step in enumerate((-1, 1)):
            at = here[k] + step
            there = jnp.logical_and(at >= 0, at < counts[k])
            at = jnp.clip(at, 0, counts[k] - 1)
            faces.append((k, side, axis, at, there))
            pl.when(there)(lambda axis=axis, at=at: pl.semaphore_signal(
                barrier, inc=1, device_id={axis: at}, device_id_type=mesh_id))
            expected = expected + there.astype(jnp.int32)
    pl.semaphore_wait(barrier, expected)
    swap = pltpu.make_async_remote_copy(
        src_ref=sent_ref, dst_ref=back, send_sem=sems.at[0, 2, 0, 0], recv_sem=sems.at[0, 2, 1, 0],
        device_id={"gx": mate}, device_id_type=mesh_id)
    swap.start()
    halos = (xh, yh, zh)
    for k, side, axis, at, there in faces:
        @pl.when(jnp.logical_not(there))
        def _():
            for r in range(SWEEPS):
                halos[k][r, side] = jnp.zeros(halos[k].shape[2:], f32)
    size_x, size_y, size_z = m.shape[2:]
    lanes = zh.shape[-1]
    weight = OMEGA * flag_ref[...].astype(f32)
    origin = [at.astype(f32) + 0.5 for at in here]
    own_tiles(pos_ref, coef_ref, features, parts, origin)
    per = TILE // size_z
    early = first_ref.shape[0]
    for t in range(early + LATE):
        if t < early:
            both = first_ref[t]
        else:
            s = slot_ref[2, t]
            both = merged(pair_sum(node_features(x_ref, t, origin), features[s], parts[s]))
        for j in range(per):
            at = t * per + j
            rbf[:, at // size_y, at % size_y, :] = both[3:6, j * size_z : (j + 1) * size_z]
    rows = lax.broadcasted_iota(jnp.int32, (size_x, size_y, size_z), 1)
    cols = lax.broadcasted_iota(jnp.int32, (size_x, size_y, size_z), 2)
    swap.wait()
    now = [rbf[c] + (mine_ref[c] + back[c]) for c in range(3)]
    for r in range(SWEEPS):
        for c in range(3):
            m[r, c] = now[c]
            yface[r, 0, c] = now[c][:, 0, :]
            yface[r, 1, c] = now[c][:, size_y - 1, :]
        copies = []
        for k, side, axis, at, there in faces:
            if k == 0:
                src = m.at[r, :, (size_x - 1) * side]
            elif k == 1:
                src = yface.at[r, side]
            else:
                src = m.at[r, :, :, :, pl.ds((size_z - lanes) * side, lanes)]
            out = pltpu.make_async_remote_copy(
                src_ref=src, dst_ref=halos[k].at[r, 1 - side], send_sem=zsend.at[r, k, side],
                recv_sem=sems.at[r + 1, k, 1 - side, 0], device_id={axis: at}, device_id_type=mesh_id)
            back_in = pltpu.make_async_remote_copy(
                src_ref=src, dst_ref=halos[k].at[r, side], send_sem=zsend.at[r, k, side],
                recv_sem=sems.at[r + 1, k, side, 0], device_id={axis: at}, device_id_type=mesh_id)
            pl.when(there)(out.start)
            copies.append((out, back_in, there))
        for out, back_in, there in copies:
            pl.when(there)(back_in.wait_recv)
            pl.when(there)(out.wait_send)
        later = []
        for c in range(3):
            v = now[c]
            total = jnp.concatenate([xh[r, 0, c][None], v[:-1]], 0)
            total = total + jnp.concatenate([v[1:], xh[r, 1, c][None]], 0)
            low = jnp.broadcast_to(yh[r, 0, c][:, None, :], v.shape)
            high = jnp.broadcast_to(yh[r, 1, c][:, None, :], v.shape)
            total = total + jnp.where(rows == 0, low, pltpu.roll(v, 1, 1))
            total = total + jnp.where(rows == size_y - 1, high, pltpu.roll(v, size_y - 1, 1))
            low = pltpu.roll(zh[r, 0, c], 1, 2)
            high = pltpu.roll(zh[r, 1, c], lanes - 1, 2)
            low = jnp.concatenate([low] * (size_z // lanes), 2)
            high = jnp.concatenate([high] * (size_z // lanes), 2)
            total = total + jnp.where(cols == 0, low, pltpu.roll(v, 1, 2))
            total = total + jnp.where(cols == size_z - 1, high, pltpu.roll(v, size_z - 1, 2))
            later.append(v + weight * (total * (1.0 / 6.0) - v))
        now = later
    for c in range(3):
        o_ref[c] = now[c]


SM = pl.BlockSpec(memory_space=pltpu.SMEM)
VM = pl.BlockSpec(memory_space=pltpu.VMEM)


ANY = pl.BlockSpec(memory_space=pl.ANY)


def gather_call(axes, half, nodes, pos, coef, pairs, live):
    ntiles = nodes.shape[1] * nodes.shape[2] // TILE
    spans = [len(shifts) for _, shifts, _ in axes]
    widest = max(spans)
    return pl.pallas_call(
        functools.partial(gather_kernel, axes, half),
        out_shape=(
            jax.ShapeDtypeStruct((ntiles - LATE, 8, TILE), f32),
            jax.ShapeDtypeStruct((spans[2], spans[1], spans[0], CT - 1, 8, TILE), f32),
            jax.ShapeDtypeStruct((2,) + nodes.shape, f32),
            jax.ShapeDtypeStruct((8, pairs.shape[1]), jnp.int32),
        ),
        in_specs=[SM, SM, VM, VM, VM, VM],
        out_specs=(VM, ANY, ANY, ANY),
        scratch_shapes=[
            pltpu.VMEM((CT - 1, 8, TILE), f32),
            pltpu.VMEM((8, pairs.shape[1]), jnp.int32),
            pltpu.SemaphoreType.DMA((3, widest, spans[0] * spans[1])),
            pltpu.SemaphoreType.DMA((3, widest, spans[0] * spans[1])),
            pltpu.SemaphoreType.DMA((2, 2)),
            pltpu.SemaphoreType.DMA((2,)),
            pltpu.VMEM((CT, TILE, 48), bf16),
            pltpu.VMEM((CT, 16, TILE), bf16),
        ],
        compiler_params=pltpu.CompilerParams(collective_id=0, has_side_effects=True),
        name="gather",
    )(pairs, live, nodes, pos, coef, pairs)


def rest_call(axes, half, pairs, live, mate_meta, x_both, table):
    ntiles = x_both.shape[2] * x_both.shape[3] // TILE
    shape = jax.ShapeDtypeStruct(x_both.shape[1:], f32)
    return pl.pallas_call(
        functools.partial(rest_kernel, axes, half),
        out_shape=(shape, shape),
        in_specs=[SM, SM, SM, VM, VM],
        out_specs=(VM, VM),
        scratch_shapes=[pltpu.VMEM((2 * ntiles + 1, 16, TILE), f32)],
        name="rest",
    )(pairs, live, mate_meta, x_both, table)


def smooth_call(half, pairs, nodes, pos, coef, first, sent, mine, flags):
    shape = mine.shape
    _, size_x, size_y, size_z = shape
    lanes = min(128, size_z)
    return pl.pallas_call(
        functools.partial(smooth_kernel, half),
        out_shape=jax.ShapeDtypeStruct(shape, f32),
        in_specs=[SM] + [VM] * 7,
        out_specs=VM,
        scratch_shapes=[
            pltpu.VMEM(shape, f32),
            pltpu.VMEM((SWEEPS,) + shape, f32),
            pltpu.VMEM((SWEEPS, 2, 3, size_x, size_z), f32),
            pltpu.VMEM((SWEEPS, 2, 3, size_y, size_z), f32),
            pltpu.VMEM((SWEEPS, 2, 3, size_x, size_z), f32),
            pltpu.VMEM((SWEEPS, 2, 3, size_x, size_y, lanes), f32),
            pltpu.SemaphoreType.DMA((SWEEPS + 1, 3, 2, 1)),
            pltpu.SemaphoreType.DMA((SWEEPS, 3, 2)),
            pltpu.VMEM((CT, TILE, 48), bf16),
            pltpu.VMEM((CT, 16, TILE), bf16),
            pltpu.VMEM(shape, f32),
        ],
        compiler_params=pltpu.CompilerParams(collective_id=1, has_side_effects=True),
        name="smooth",
    )(pairs, nodes, pos, coef, first, sent, mine, flags)


def offsets(count, wanted):
    seen = []
    for d in wanted:
        if d % count not in seen:
            seen.append(d % count)
    return seen


def on_device(
    node_positions,
    control_positions,
    control_coefficient_values,
    support_pairs,
    live_counts,
    sliver_flags,
):
    size_x, size_y, size_z = node_positions.shape[1:]
    nx, ny, nz = (lax.axis_size(a) for a in ("gx", "gy", "gz"))
    half = nx // 2
    nodes = node_positions.reshape(3, size_x * size_y, size_z)
    axes = (
        ("gx", offsets(nx, (0, 1, -1, half, half + 1, half - 1)), True),
        ("gy", offsets(ny, (0, 1, -1)), ny <= 2),
        ("gz", offsets(nz, (0, 1, -1)), nz <= 2),
    )
    pairs = support_pairs.T
    first, table, x_both, mate_meta = gather_call(
        axes, half, nodes, control_positions, control_coefficient_values, pairs, live_counts
    )
    table = table.reshape((-1,) + table.shape[4:])
    sent, mine = rest_call(axes, half, pairs, live_counts, mate_meta, x_both, table)
    shape = node_positions.shape
    return smooth_call(
        half, pairs, nodes, control_positions, control_coefficient_values, first,
        sent.reshape(shape), mine.reshape(shape), sliver_flags,
    )


def solution(mesh):
    return jax.shard_map(
        on_device,
        mesh=mesh,
        in_specs=(
            P(None, "gx", "gy", "gz"),
            P(None, ("gx", "gy", "gz")),
            P(None, ("gx", "gy", "gz")),
            P(("gx", "gy", "gz"), None),
            P(("gx", "gy", "gz")),
            P("gx", "gy", "gz"),
        ),
        out_specs=P(None, "gx", "gy", "gz"),
        check_vma=False,
    )
```

```python
import functools

import jax
import jax.numpy as jnp
from jax import lax
from jax.experimental import pallas as pl
from jax.experimental.pallas import tpu as pltpu
from jax.sharding import PartitionSpec as P

TILE = 512
CT = 4
PAIRS = 128
SWEEPS = 2
RADIUS = 1.5
OMEGA = 0.7
GROUP = 8
STEP = 4
LATE = 12
HALF = 256
FLOOR = 2.0**-21
bf16, f32 = jnp.bfloat16, jnp.float32


def split3(x):
    a = x.astype(bf16).astype(f32)
    r = x - a
    b = r.astype(bf16).astype(f32)
    return a, b, r - b


def row_ids():
    return lax.broadcasted_iota(jnp.int32, (8, TILE), 0)


def node_features(x_ref, t, origin):
    per = TILE // x_ref.shape[2]
    rows = row_ids()
    coords = []
    for c in range(3):
        row = jnp.concatenate(
            [x_ref[c, pl.ds(t * per + j, 1), :] for j in range(per)], axis=1
        )
        coords.append((row - origin[c]) * (1.0 / RADIUS))
    norm = coords[0] * coords[0] + coords[1] * coords[1] + coords[2] * coords[2]
    block = jnp.where(rows == 4, 1.0, 0.0)
    for i, row in enumerate(coords + [norm]):
        block = jnp.where(rows == i, jnp.broadcast_to(row, (8, TILE)), block)
    a, b, c = split3(block)
    return jnp.concatenate([a, a, b, b, a, c], 0).astype(bf16)


def control_features(raw, origin):
    rows = row_ids()
    shift = jnp.where(rows == 0, origin[0], jnp.where(rows == 1, origin[1], origin[2]))
    pos = jnp.where(rows < 3, (raw - shift) * (1.0 / RADIUS), 0.0)
    norm = jnp.sum(pos * pos, axis=0, keepdims=True) + FLOOR
    block = jnp.where(rows == 3, 1.0, -2.0 * pos)
    block = jnp.where(rows == 4, jnp.broadcast_to(norm, (8, TILE)), block)
    a, b, c = split3(block)
    return jnp.transpose(jnp.concatenate([a, b, a, b, c, a], 0)).astype(bf16)


def coef_parts(raw):
    high = raw.astype(bf16).astype(f32)
    return jnp.concatenate([high, raw - high], 0).astype(bf16)


def pair_sum(nodes, controls, coefs):
    coefs = jnp.concatenate([coefs, coefs], 1)
    sums = []
    for n in range(0, TILE, HALF):
        dist_sq = jnp.dot(controls, nodes[:, n : n + HALF], preferred_element_type=f32)
        scaled = dist_sq * lax.rsqrt(dist_sq)
        fall = jnp.maximum(1.0 - scaled, 0.0)
        fall2 = fall * fall
        weight = (fall2 * fall2) * (0.25 + scaled)
        top = weight.astype(bf16)
        rest = (weight - top.astype(f32)).astype(bf16)
        sums.append(
            jnp.dot(coefs, jnp.concatenate([top, rest], 0), preferred_element_type=f32)
        )
    return jnp.concatenate(sums, 1)


def own_tiles(pos_ref, coef_ref, features, parts, origin):
    for s in range(CT):
        at = slice(s * TILE, (s + 1) * TILE)
        raw = jnp.concatenate([pos_ref[:, at], coef_ref[:, at], jnp.zeros((2, TILE), f32)], 0)
        features[s] = control_features(raw, origin)
        parts[s] = coef_parts(raw)


def pack_tiles(pos_ref, coef_ref, own_ref):
    last = slice((CT - 1) * TILE, CT * TILE)
    for s in range(CT - 1):
        at = slice(s * TILE, (s + 1) * TILE)
        own_ref[s, 0:3] = pos_ref[:, at]
        own_ref[s, 3:6] = coef_ref[:, at]
        for j in range(2):
            c = 2 * s + j
            own_ref[s, 6 + j : 7 + j] = pos_ref[c : c + 1, last] if c < 3 else coef_ref[c - 3 : c - 2, last]


def tile_rows(table, block, slot):
    whole = table[block + (jnp.minimum(slot, CT - 2),)]
    last = jnp.concatenate([table[block + (s, slice(6, 8))] for s in range(CT - 1)] + [jnp.zeros((2, TILE), f32)], 0)
    return jnp.where(slot == CT - 1, last, whole)


def merged(both):
    return 4.0 * (both[:8] + both[8:])


def peers(axis, shifts, wrap):
    count, me = lax.axis_size(axis), lax.axis_index(axis)
    for i, d in enumerate(shifts):
        if d == 0:
            continue
        step = d if wrap or d == 1 else d - count
        ahead = None if wrap else jnp.logical_and(me + step >= 0, me + step < count)
        behind = None if wrap else jnp.logical_and(me - step >= 0, me - step < count)
        yield i, (me + step + count) % count, (me - step + count) % count, ahead, behind


def both_of(a, b):
    if a is None or b is None:
        return b if a is None else a
    return jnp.logical_and(a, b)


def when(cond, do):
    if cond is None:
        do()
    else:
        pl.when(cond)(do)


def gather_kernel(axes, half, slot_ref, live_ref, x_ref, pos_ref, coef_ref, pairs_ref, o_ref, table, x_both, mate_meta, own_ref, meta_ref, send, recv, extra, local, features, parts):
    origin = [lax.axis_index(axis).astype(f32) + 0.5 for axis, _, _ in axes]
    barrier = pltpu.get_barrier_semaphore()
    expected = 0
    for axis, shifts, wrap in axes:
        for _, ahead, _, there, _ in peers(axis, shifts, wrap):
            when(there, lambda axis=axis, ahead=ahead: pl.semaphore_signal(
                barrier, inc=1, device_id={axis: ahead}, device_id_type=pl.DeviceIdType.MESH))
            expected = expected + (1 if there is None else there.astype(jnp.int32))
    meta_ref[0:3] = pairs_ref[...]
    meta_ref[3:8] = jnp.full((5, meta_ref.shape[1]), live_ref[0], jnp.int32)
    pack_tiles(pos_ref, coef_ref, own_ref)
    pl.semaphore_wait(barrier, expected)

    wide = [len(shifts) for _, shifts, _ in axes]
    columns = [(i1, i0) for i1 in range(wide[1]) for i0 in range(wide[0])]
    came = {0: None}
    for i, _, _, has_ahead, _ in peers(*axes[1]):
        came[i] = has_ahead

    def copies(k, blocks, only=None):
        axis, shifts, wrap = axes[k]
        for i, ahead, behind, has_ahead, has_behind in peers(axis, shifts, wrap):
            for i1, i0 in blocks if only is None or i in only else ():
                src = table.at[0, i1, i0] if i1 or i0 else own_ref
                dst = table.at[(0, 0, i) if k == 0 else (0, i, i0) if k == 1 else (i, i1, i0)]
                n = i1 * wide[0] + i0
                copy = pltpu.make_async_remote_copy(
                    src_ref=src, dst_ref=dst, send_sem=send.at[k, i, n], recv_sem=recv.at[k, i, n],
                    device_id={axis: behind}, device_id_type=pl.DeviceIdType.MESH)
                yield copy, both_of(has_behind, came[i1]), both_of(has_ahead, came[i1])

    def start(k, blocks):
        for copy, goes, _ in copies(k, blocks):
            when(goes, copy.start)

    def land(k, blocks, only=None):
        for copy, _, comes in copies(k, blocks, only):
            when(comes, copy.wait_recv)

    def drain(k, blocks):
        for copy, goes, _ in copies(k, blocks):
            when(goes, copy.wait_send)

    def relay(i0):
        land(0, near, (i0,))
        start(1, [(0, i0)])
        start(2, [(0, i0)])

    near = [(0, 0)]
    row = [(0, i0) for i0 in range(1, wide[0])]
    side = [(i1, 0) for i1 in range(1, wide[1])]

    gx_name = axes[0][0]
    count = lax.axis_size(gx_name)
    mate = (lax.axis_index(gx_name) + half) % count
    keep = [
        pltpu.make_async_copy(own_ref, table.at[0, 0, 0], local.at[0]),
        pltpu.make_async_copy(x_ref, x_both.at[1], local.at[1]),
    ]
    for k in range(3):
        start(k, near)
    for copy in keep:
        copy.start()
    swaps = [
        pltpu.make_async_remote_copy(
            src_ref=src, dst_ref=dst, send_sem=extra.at[0, n], recv_sem=extra.at[1, n],
            device_id={gx_name: mate}, device_id_type=pl.DeviceIdType.MESH)
        for n, (src, dst) in enumerate(((meta_ref, mate_meta), (x_ref, x_both.at[0])))
    ]
    swaps[0].start()

    own_tiles(pos_ref, coef_ref, features, parts, origin)
    groups = o_ref.shape[0] // STEP
    direct = [i for i, d in enumerate(axes[0][1]) if d == half]
    others = [i for i in range(1, wide[0]) if i not in direct]

    @pl.loop(0, groups)
    def _(g):
        for j in range(STEP):
            i = g * STEP + j
            s = slot_ref[2, i]
            o_ref[i] = merged(pair_sum(node_features(x_ref, i, origin), features[s], parts[s]))

        @pl.when(g == 1)
        def _():
            for i0 in direct + others:
                relay(i0)
            swaps[1].start()
            for copy in keep:
                copy.wait()
            land(1, near)
            start(2, side)

        @pl.when(g == 3)
        def _():
            for i0 in direct + others:
                land(1, [(0, i0)])
                start(2, [(i1, i0) for i1 in range(1, wide[1])])

    land(2, columns)
    drain(0, near)
    drain(1, near + row)
    drain(2, columns)
    for copy in swaps:
        copy.wait()


def finish(acc, at, o_ref):
    _, size_x, size_y, width = o_ref.shape
    per = TILE // width
    for t in range(size_x * size_y // per):
        both = merged(acc[at + t])
        for j in range(per):
            at_row = t * per + j
            o_ref[:, at_row // size_y, at_row % size_y, :] = both[3:6, j * width : (j + 1) * width]


def rest_kernel(axes, half, meta, live, mate_meta, x_both, table, sent_ref, o_ref, acc):
    trash = acc.shape[0] - 1
    ntiles = trash // 2
    acc[:trash] = jnp.zeros((trash,) + acc.shape[1:], f32)
    here = [lax.axis_index(axis) for axis, _, _ in axes]
    counts = [lax.axis_size(axis) for axis, _, _ in axes]
    mate_at = lax.rem(here[0] + half, counts[0])
    mine, theirs = live[0], mate_meta[3, 0]
    goal = lax.div(mine + theirs + 1, 2)
    skip = jnp.minimum(goal, theirs)
    helped = theirs - skip
    total = helped + jnp.minimum(mine, goal) - ntiles

    def source(owner):
        owners = (
            lax.div(owner, counts[1] * counts[2]),
            lax.rem(lax.div(owner, counts[2]), counts[1]),
            lax.rem(owner, counts[2]),
        )
        at = ()
        for k in (2, 1, 0):
            shifts = axes[k][1]
            rel = lax.rem(owners[k] - here[k] + counts[k], counts[k])
            at = at + (sum(jnp.where(rel == d, i, 0) for i, d in enumerate(shifts)),)
        return at

    @pl.loop(0, lax.div(total + GROUP - 1, GROUP))
    def _(g):
        for j in range(GROUP):
            p = g * GROUP + j
            for_mate = p < helped
            slot = jnp.minimum(jnp.where(for_mate, skip + p, ntiles + p - helped), PAIRS - 1)
            t, owner, tile = (
                jnp.where(for_mate, mate_meta[c, slot], meta[c, slot]) for c in range(3)
            )
            part = jnp.where(for_mate, 0, 1)
            origin = [
                jnp.where(for_mate, mate_at, here[0]).astype(f32) + 0.5,
                here[1].astype(f32) + 0.5,
                here[2].astype(f32) + 0.5,
            ]
            nodes = node_features(x_both.at[part], t, origin)
            into = jnp.where(p < total, part * ntiles + t, trash)
            raw = tile_rows(table, source(owner), tile)
            acc[into] += pair_sum(nodes, control_features(raw, origin), coef_parts(raw))

    finish(acc, 0, sent_ref)
    finish(acc, ntiles, o_ref)


def smooth_kernel(half, slot_ref, x_ref, pos_ref, coef_ref, first_ref, sent_ref, mine_ref, flag_ref, o_ref, back, m, yface, xh, yh, zh, sems, zsend, features, parts, rbf):
    names = ("gx", "gy", "gz")
    here = [lax.axis_index(a) for a in names]
    counts = [lax.axis_size(a) for a in names]
    mate = (here[0] + half) % counts[0]
    mesh_id = pl.DeviceIdType.MESH
    barrier = pltpu.get_barrier_semaphore()
    pl.semaphore_signal(barrier, inc=1, device_id={"gx": mate}, device_id_type=mesh_id)
    expected = 1
    faces = []
    for k, axis in enumerate(names):
        for side, step in enumerate((-1, 1)):
            at = here[k] + step
            there = jnp.logical_and(at >= 0, at < counts[k])
            at = jnp.clip(at, 0, counts[k] - 1)
            faces.append((k, side, axis, at, there))
            pl.when(there)(lambda axis=axis, at=at: pl.semaphore_signal(
                barrier, inc=1, device_id={axis: at}, device_id_type=mesh_id))
            expected = expected + there.astype(jnp.int32)
    pl.semaphore_wait(barrier, expected)
    swap = pltpu.make_async_remote_copy(
        src_ref=sent_ref, dst_ref=back, send_sem=sems.at[0, 2, 0, 0], recv_sem=sems.at[0, 2, 1, 0],
        device_id={"gx": mate}, device_id_type=mesh_id)
    swap.start()
    halos = (xh, yh, zh)
    for k, side, axis, at, there in faces:
        @pl.when(jnp.logical_not(there))
        def _():
            for r in range(SWEEPS):
                halos[k][r, side] = jnp.zeros(halos[k].shape[2:], f32)
    size_x, size_y, size_z = m.shape[2:]
    lanes = zh.shape[-1]
    weight = OMEGA * flag_ref[...].astype(f32)
    origin = [at.astype(f32) + 0.5 for at in here]
    own_tiles(pos_ref, coef_ref, features, parts, origin)
    per = TILE // size_z
    early = first_ref.shape[0]
    for t in range(early + LATE):
        if t < early:
            both = first_ref[t]
        else:
            s = slot_ref[2, t]
            both = merged(pair_sum(node_features(x_ref, t, origin), features[s], parts[s]))
        for j in range(per):
            at = t * per + j
            rbf[:, at // size_y, at % size_y, :] = both[3:6, j * size_z : (j + 1) * size_z]
    rows = lax.broadcasted_iota(jnp.int32, (size_x, size_y, size_z), 1)
    cols = lax.broadcasted_iota(jnp.int32, (size_x, size_y, size_z), 2)
    swap.wait()
    now = [rbf[c] + (mine_ref[c] + back[c]) for c in range(3)]
    for r in range(SWEEPS):
        for c in range(3):
            m[r, c] = now[c]
            yface[r, 0, c] = now[c][:, 0, :]
            yface[r, 1, c] = now[c][:, size_y - 1, :]
        copies = []
        for k, side, axis, at, there in faces:
            if k == 0:
                src = m.at[r, :, (size_x - 1) * side]
            elif k == 1:
                src = yface.at[r, side]
            else:
                src = m.at[r, :, :, :, pl.ds((size_z - lanes) * side, lanes)]
            out = pltpu.make_async_remote_copy(
                src_ref=src, dst_ref=halos[k].at[r, 1 - side], send_sem=zsend.at[r, k, side],
                recv_sem=sems.at[r + 1, k, 1 - side, 0], device_id={axis: at}, device_id_type=mesh_id)
            back_in = pltpu.make_async_remote_copy(
                src_ref=src, dst_ref=halos[k].at[r, side], send_sem=zsend.at[r, k, side],
                recv_sem=sems.at[r + 1, k, side, 0], device_id={axis: at}, device_id_type=mesh_id)
            pl.when(there)(out.start)
            copies.append((out, back_in, there))
        for out, back_in, there in copies:
            pl.when(there)(back_in.wait_recv)
            pl.when(there)(out.wait_send)
        later = []
        for c in range(3):
            v = now[c]
            total = jnp.concatenate([xh[r, 0, c][None], v[:-1]], 0)
            total = total + jnp.concatenate([v[1:], xh[r, 1, c][None]], 0)
            low = jnp.broadcast_to(yh[r, 0, c][:, None, :], v.shape)
            high = jnp.broadcast_to(yh[r, 1, c][:, None, :], v.shape)
            total = total + jnp.where(rows == 0, low, pltpu.roll(v, 1, 1))
            total = total + jnp.where(rows == size_y - 1, high, pltpu.roll(v, size_y - 1, 1))
            low = pltpu.roll(zh[r, 0, c], 1, 2)
            high = pltpu.roll(zh[r, 1, c], lanes - 1, 2)
            low = jnp.concatenate([low] * (size_z // lanes), 2)
            high = jnp.concatenate([high] * (size_z // lanes), 2)
            total = total + jnp.where(cols == 0, low, pltpu.roll(v, 1, 2))
            total = total + jnp.where(cols == size_z - 1, high, pltpu.roll(v, size_z - 1, 2))
            later.append(v + weight * (total * (1.0 / 6.0) - v))
        now = later
    for c in range(3):
        o_ref[c] = now[c]


SM = pl.BlockSpec(memory_space=pltpu.SMEM)
VM = pl.BlockSpec(memory_space=pltpu.VMEM)


ANY = pl.BlockSpec(memory_space=pl.ANY)
HELD = pltpu.VMEM


def held(*arrays):
    return tuple(pltpu.with_memory_space_constraint(x, pltpu.VMEM) for x in arrays)


def gather_call(axes, half, nodes, pos, coef, pairs, live):
    ntiles = nodes.shape[1] * nodes.shape[2] // TILE
    spans = [len(shifts) for _, shifts, _ in axes]
    widest = max(spans)
    return pl.pallas_call(
        functools.partial(gather_kernel, axes, half),
        out_shape=(
            HELD((ntiles - LATE, 8, TILE), f32),
            HELD((spans[2], spans[1], spans[0], CT - 1, 8, TILE), f32),
            HELD((2,) + nodes.shape, f32),
            jax.ShapeDtypeStruct((8, pairs.shape[1]), jnp.int32),
        ),
        in_specs=[SM, SM, VM, VM, VM, VM],
        out_specs=(VM, VM, VM, ANY),
        scratch_shapes=[
            pltpu.VMEM((CT - 1, 8, TILE), f32),
            pltpu.VMEM((8, pairs.shape[1]), jnp.int32),
            pltpu.SemaphoreType.DMA((3, widest, spans[0] * spans[1])),
            pltpu.SemaphoreType.DMA((3, widest, spans[0] * spans[1])),
            pltpu.SemaphoreType.DMA((2, 2)),
            pltpu.SemaphoreType.DMA((2,)),
            pltpu.VMEM((CT, TILE, 48), bf16),
            pltpu.VMEM((CT, 16, TILE), bf16),
        ],
        compiler_params=pltpu.CompilerParams(collective_id=0, has_side_effects=True),
        name="gather",
    )(pairs, live, nodes, pos, coef, pairs)


def rest_call(axes, half, pairs, live, mate_meta, x_both, table, block):
    ntiles = x_both.shape[2] * x_both.shape[3] // TILE
    shape = HELD(block, f32)
    return pl.pallas_call(
        functools.partial(rest_kernel, axes, half),
        out_shape=(shape, shape),
        in_specs=[SM, SM, SM, VM, VM],
        out_specs=(VM, VM),
        scratch_shapes=[pltpu.VMEM((2 * ntiles + 1, 16, TILE), f32)],
        name="rest",
    )(pairs, live, mate_meta, *held(x_both, table))


def smooth_call(half, pairs, nodes, pos, coef, first, sent, mine, flags):
    shape = mine.shape
    _, size_x, size_y, size_z = shape
    lanes = min(128, size_z)
    return pl.pallas_call(
        functools.partial(smooth_kernel, half),
        out_shape=HELD(shape, f32),
        in_specs=[SM] + [VM] * 7,
        out_specs=VM,
        scratch_shapes=[
            pltpu.VMEM(shape, f32),
            pltpu.VMEM((SWEEPS,) + shape, f32),
            pltpu.VMEM((SWEEPS, 2, 3, size_x, size_z), f32),
            pltpu.VMEM((SWEEPS, 2, 3, size_y, size_z), f32),
            pltpu.VMEM((SWEEPS, 2, 3, size_x, size_z), f32),
            pltpu.VMEM((SWEEPS, 2, 3, size_x, size_y, lanes), f32),
            pltpu.SemaphoreType.DMA((SWEEPS + 1, 3, 2, 1)),
            pltpu.SemaphoreType.DMA((SWEEPS, 3, 2)),
            pltpu.VMEM((CT, TILE, 48), bf16),
            pltpu.VMEM((CT, 16, TILE), bf16),
            pltpu.VMEM(shape, f32),
        ],
        compiler_params=pltpu.CompilerParams(collective_id=1, has_side_effects=True),
        name="smooth",
    )(pairs, nodes, pos, coef, *held(first, sent, mine), flags)


def store_kernel(x_ref, o_ref, sem):
    copy = pltpu.make_async_copy(x_ref, o_ref, sem)
    copy.start()
    copy.wait()


def store_call(moved):
    return pl.pallas_call(
        store_kernel,
        out_shape=jax.ShapeDtypeStruct(moved.shape, f32),
        in_specs=[VM],
        out_specs=ANY,
        scratch_shapes=[pltpu.SemaphoreType.DMA],
        name="store",
    )(*held(moved))


def offsets(count, wanted):
    seen = []
    for d in wanted:
        if d % count not in seen:
            seen.append(d % count)
    return seen


def on_device(
    node_positions,
    control_positions,
    control_coefficient_values,
    support_pairs,
    live_counts,
    sliver_flags,
):
    size_x, size_y, size_z = node_positions.shape[1:]
    nx, ny, nz = (lax.axis_size(a) for a in ("gx", "gy", "gz"))
    half = nx // 2
    nodes = node_positions.reshape(3, size_x * size_y, size_z)
    axes = (
        ("gx", offsets(nx, (0, 1, -1, half, half + 1, half - 1)), True),
        ("gy", offsets(ny, (0, 1, -1)), ny <= 2),
        ("gz", offsets(nz, (0, 1, -1)), nz <= 2),
    )
    pairs = support_pairs.T
    first, table, x_both, mate_meta = gather_call(
        axes, half, nodes, control_positions, control_coefficient_values, pairs, live_counts
    )
    shape = node_positions.shape
    sent, mine = rest_call(axes, half, pairs, live_counts, mate_meta, x_both, table, shape)
    moved = smooth_call(
        half, pairs, nodes, control_positions, control_coefficient_values, first,
        sent, mine, sliver_flags,
    )
    return store_call(moved)


def solution(mesh):
    return jax.shard_map(
        on_device,
        mesh=mesh,
        in_specs=(
            P(None, "gx", "gy", "gz"),
            P(None, ("gx", "gy", "gz")),
            P(None, ("gx", "gy", "gz")),
            P(("gx", "gy", "gz"), None),
            P(("gx", "gy", "gz")),
            P("gx", "gy", "gz"),
        ),
        out_specs=P(None, "gx", "gy", "gz"),
        check_vma=False,
    )
```
